256 devices in a mesh: seq: 32 (over y, z), nb: 8 (over x, core).
Axes of the slice: x: 4, y: 4, z: 8, core: 2. Of those that a mesh axis runs over, the one named last changes fastest.
Arguments:
- q_self: bfloat16 [8192, 4096], P('seq', 'nb'), may hold values from -6 to 6
- k_self: bfloat16 [8192, 4096], P('seq', 'nb'), may hold values from -6 to 6
- v_self: bfloat16 [8192, 4096], P('seq', 'nb'), may hold values from -6 to 6
- q_cca: bfloat16 [8192, 4096], P('seq', 'nb'), may hold values from -6 to 6
- memory: bfloat16 [8192, 2, 1024], P('seq'), may hold values from -6 to 6
- database: bfloat16 [65536, 2048], P(('seq', 'nb')), may hold values from -6 to 6
- nbr_block: int32 [2048], P(('seq', 'nb')), may hold values from 0 to 127, as said below
- span_offset: int32 [128], P('seq'), may hold values from 1 to 63
- enc_query: bfloat16 [2048, 1024], P('seq'), may hold values from -0.1355122 to 0.1355122
- enc_out: bfloat16 [1024, 2048], P('seq'), may hold values from -0.1875 to 0.1875
- enc_gain: float32 [2048], replicated, may hold values from 0.5 to 1.5
- cca_kv: bfloat16 [2048, 2, 4096], P(None, None, 'nb'), may hold values from -0.134535646 to 0.134535646
Outputs:
- attended: bfloat16 [8192, 4096], P('seq', 'nb')
The draws below stay inside these ranges and needn't reach their ends.
Inputs may be any that keep to these rules, and one draw needn't show every extreme that they name: `nbr_block`: block ids are local to a group of 8 devices along nb; the owner of id g is nb index g // 16. Among the 8 requests of one device at most 3 name blocks of one owner, and exactly 3 name blocks of some owner.
All inputs are finite; a program needn't handle non-finite values.
Results may differ from the reference program's by a relative error of at most 0.0041.
Values may be sent and summed in bfloat16 or wider, within the bound.
No kernel may reach another device: no remote copies, remote signals or barrier semaphores. Data moves between devices by JAX's collectives and lax.ppermute only.
A program may use at most 192 MiB of HBM per device.

```python
import jax
import jax.numpy as jnp
from jax import lax

HD = 128
HEADS = 32
E = 2048
EH = 8
SPAN = 64
K = 2
R = 128
BLK = 16
DB_DEV = 16
TOKENS = 8192
SPANS = 128
REQ_DEV = 8
REQUESTS = 2048
CAP = 3
DB_ROWS = 65536
N_NB = 8


def base_field(key, shape):
    return jnp.clip(jax.random.normal(key, shape, jnp.float32), -6.0, 6.0)


def sign_table(key, tag, shape):
    bits = jax.random.randint(jax.random.fold_in(key, tag), shape, 0, 2)
    return (2 * bits - 1).astype(jnp.float32)


def planted_queries(key, tag, strength_lo, strength_hi):
    signs = sign_table(key, tag, (HEADS, HD))
    rows = jnp.arange(TOKENS, dtype=jnp.int32)
    chosen = jax.random.randint(jax.random.fold_in(key, tag + 1), (TOKENS,), 0, 64) == 0
    chosen = chosen & (rows >= 8) | (rows == TOKENS - 1)
    head_pick = jax.random.randint(jax.random.fold_in(key, tag + 2), (TOKENS,), 0, HEADS)
    strength = jax.random.uniform(jax.random.fold_in(key, tag + 3), (TOKENS,), jnp.float32, strength_lo, strength_hi)
    strength = jnp.where(rows == TOKENS - 1, strength_hi, strength)
    head_hit = (head_pick[:, None] == jnp.arange(HEADS, dtype=jnp.int32)[None, :]) & chosen[:, None]
    planted = strength[:, None, None] * signs[None, :, :]
    return (head_hit, planted)


def draw_q_self(key, part):
    base = base_field(jax.random.fold_in(key, 1), (TOKENS, HEADS, HD))
    head_hit, planted = planted_queries(key, 201, 2.4, 5.4)
    return jnp.where(head_hit[:, :, None], planted, base).reshape(TOKENS, HEADS * HD).astype(jnp.bfloat16)


def draw_k_self(key, part):
    base = base_field(jax.random.fold_in(key, 2), (TOKENS, HEADS, HD))
    signs = sign_table(key, 201, (HEADS, HD))
    first = jax.random.randint(jax.random.fold_in(key, 211), (), 0, 8)
    second = (first + 1 + jax.random.randint(jax.random.fold_in(key, 212), (), 0, 7)) % 8
    rows = jnp.arange(TOKENS, dtype=jnp.int32)[:, None, None]
    field = jnp.where(rows == second, 3.953125 * signs[None], base)
    field = jnp.where(rows == first, 4.0 * signs[None], field)
    return field.reshape(TOKENS, HEADS * HD).astype(jnp.bfloat16)


def draw_q_cca(key, part):
    base = base_field(jax.random.fold_in(key, 3), (TOKENS, HEADS, HD))
    head_hit, planted = planted_queries(key, 301, 2.4, 5.5)
    return jnp.where(head_hit[:, :, None], planted, base).reshape(TOKENS, HEADS * HD).astype(jnp.bfloat16)


def draw_memory(key, part):
    base = base_field(jax.random.fold_in(key, 4), (TOKENS, 2, EH, HD))
    signs = sign_table(key, 402, (EH, HD))
    span_count = TOKENS // SPAN
    level = 2.0 + jax.random.randint(jax.random.fold_in(key, 403), (span_count,), 0, 128).astype(jnp.float32) / 64.0
    level = jnp.where(jnp.arange(span_count, dtype=jnp.int32) == 0, 3.984375, level)
    second = 1 + jax.random.randint(jax.random.fold_in(key, 404), (span_count,), 0, min(7, SPAN - 1))
    rows = jnp.arange(TOKENS, dtype=jnp.int32)
    within = rows % SPAN
    row_level = jnp.repeat(level, SPAN)
    row_second = jnp.repeat(second, SPAN)
    key_level = jnp.where(within == 0, row_level, row_level - 0.03125)
    planted = (within == 0) | (within == row_second)
    keys = jnp.where(planted[:, None, None], key_level[:, None, None] * signs[None], base[:, 0])
    return jnp.stack([keys, base[:, 1]], axis=1).reshape(TOKENS, 2, EH * HD).astype(jnp.bfloat16)


def draw_database(key, part):
    base = base_field(jax.random.fold_in(key, 5), (DB_ROWS, E))
    direction = sign_table(key, 401, (E,))
    pick = jax.random.randint(jax.random.fold_in(key, 405), (DB_ROWS // BLK,), 0, BLK)
    rows = jnp.arange(DB_ROWS, dtype=jnp.int32)
    planted = rows % BLK == jnp.repeat(pick, BLK)
    return jnp.where(planted[:, None], direction[None, :] + 0.3 * base, base).astype(jnp.bfloat16)


def draw_enc_query(key, part):
    base = base_field(jax.random.fold_in(key, 6), (E, EH * HD)) * E ** (-0.5)
    direction = sign_table(key, 401, (E,))
    head_signs = sign_table(key, 402, (EH, HD)).reshape(EH * HD)
    return (base + 6.0 / E * direction[:, None] * head_signs[None, :]).astype(jnp.bfloat16)


def draw_cca_kv(key, part):
    base = base_field(jax.random.fold_in(key, 7), (E, 2, HEADS * HD)) * E ** (-0.5)
    direction = sign_table(key, 401, (E,))
    head_signs = sign_table(key, 301, (HEADS, HD)).reshape(HEADS * HD)
    keys = base[:, 0] + 4.0 / E * direction[:, None] * head_signs[None, :]
    return jnp.stack([keys, base[:, 1]], axis=1).astype(jnp.bfloat16)


def draw_nbr_block(key, part):
    device_count = REQUESTS // REQ_DEV
    key_first = jax.random.fold_in(key, 11)
    key_second = jax.random.fold_in(key, 12)
    key_rotation = jax.random.fold_in(key, 13)
    key_order = jax.random.fold_in(key, 14)
    key_blocks = jax.random.fold_in(key, 15)
    key_labels = jax.random.fold_in(key, 16)
    hot_raw = jnp.minimum(jax.random.randint(key_first, (device_count,), 0, N_NB), jax.random.randint(key_second, (device_count,), 0, N_NB))
    relabel = jax.random.permutation(key_labels, N_NB).astype(jnp.int32)
    hot_owner = relabel[hot_raw]
    rotation = jax.random.randint(key_rotation, (device_count, 1), 0, N_NB - 1)
    column = jnp.arange(REQ_DEV, dtype=jnp.int32)[None, :]
    other_owner = (hot_owner[:, None] + 1 + (column - CAP + rotation) % (N_NB - 1)) % N_NB
    owner_ids = jnp.where(column < CAP, hot_owner[:, None], other_owner)
    order_keys = jax.random.randint(key_order, (device_count, REQ_DEV), 0, 2 ** 20) * REQ_DEV + column
    order = jnp.argsort(order_keys, axis=1, stable=True)
    owner_ids = jnp.take_along_axis(owner_ids, order, axis=1)
    block_local = jax.random.randint(key_blocks, (device_count, REQ_DEV), 0, DB_DEV)
    return (owner_ids * DB_DEV + block_local).reshape(-1).astype(jnp.int32)


def touch_ends(entries, rng, smallest, high):
    spot = [jax.random.randint(jax.random.fold_in(rng, axis), (), 0, length) for axis, length in enumerate(entries.shape)]
    main_axis = entries.shape.index(max(entries.shape))
    neighbour = spot[:main_axis] + [(spot[main_axis] + 1) % entries.shape[main_axis]] + spot[main_axis + 1:]
    return entries.at[tuple(spot)].set(smallest).at[tuple(neighbour)].set(high)


def level_of(rng, extent, pieces, least, top_value):
    factor_of = 1.0
    for dim, shards_of in pieces:
        draws = jax.random.uniform(jax.random.fold_in(jax.random.fold_in(rng, 6), dim), (shards_of,), jnp.float32, least / len(pieces), top_value / len(pieces))
        factor_of = factor_of * jnp.repeat(jnp.exp(draws), extent[dim] // shards_of).reshape((-1,) + (1,) * (len(extent) - 1 - dim))
    return factor_of


def scatter_about(rng, dims, scale, bound, pieces=(), kind=jnp.bfloat16):
    factor_of = level_of(rng, dims, pieces, -0.22, 0.18) if pieces else 1.0
    values = jax.random.normal(rng, dims, jnp.float32) * scale * factor_of
    return jnp.minimum(jnp.maximum(values, -bound), bound).astype(kind)


def setup_inputs(seed: int = 0) -> dict:
    arg_keys = jax.random.split(jax.random.key(seed), 13)
    return {
        "q_self": draw_q_self(jax.random.fold_in(arg_keys[12], 71), 0),
        "k_self": draw_k_self(jax.random.fold_in(arg_keys[12], 71), 0),
        "v_self": scatter_about(arg_keys[2], (TOKENS, HEADS * HD), 1.0, 6.0, ((0, 32), (1, 8))),
        "q_cca": draw_q_cca(jax.random.fold_in(arg_keys[12], 71), 0),
        "memory": draw_memory(jax.random.fold_in(arg_keys[12], 71), 0),
        "database": draw_database(jax.random.fold_in(arg_keys[12], 71), 0),
        "nbr_block": draw_nbr_block(jax.random.fold_in(arg_keys[12], 71), 0),
        "span_offset": touch_ends(jax.random.randint(arg_keys[7], (SPANS,), 1, SPAN), jax.random.fold_in(arg_keys[7], 1), 1, SPAN - 1).astype(jnp.int32),
        "enc_query": draw_enc_query(jax.random.fold_in(arg_keys[12], 71), 0),
        "enc_out": scatter_about(arg_keys[9], (EH * HD, E), (EH * HD) ** -0.5, 0.1875, ((0, 32),)),
        "enc_gain": jnp.clip(1.0 + 0.1 * jax.random.normal(arg_keys[10], (E,), jnp.float32), 0.5, 1.5),
        "cca_kv": draw_cca_kv(jax.random.fold_in(arg_keys[12], 71), 0),
    }


masked_score = -1e+30

def reference(q_self, k_self, v_self, q_cca, memory, database, nbr_block, span_offset, enc_query, enc_out, enc_gain, cca_kv):
    score_scale = HD ** (-0.5)
    positions = jnp.arange(TOKENS, dtype=jnp.int32)
    causal = positions[:, None] >= positions[None, :]

    def self_head(operands):
        query_h, key_h, value_h = operands
        scores = jnp.dot(query_h, key_h.T, preferred_element_type=jnp.float32) * score_scale
        scores = jnp.where(causal, scores, masked_score)
        row_max = lax.optimization_barrier(jnp.max(scores, axis=1, keepdims=True))
        weights = jnp.where(causal, jnp.exp(scores - row_max), 0.0)
        totals = lax.optimization_barrier(jnp.sum(weights, axis=1, keepdims=True))
        summed = jnp.dot(weights.astype(jnp.bfloat16), value_h, preferred_element_type=jnp.float32)
        return summed / totals

    def split_heads(array):
        return array.reshape(TOKENS, HEADS, HD).transpose(1, 0, 2)
    self_out = lax.map(self_head, (split_heads(q_self), split_heads(k_self), split_heads(v_self)))
    self_out = self_out.transpose(1, 0, 2).reshape(TOKENS, HEADS * HD)
    request_ids = jnp.arange(REQUESTS, dtype=jnp.int32)
    group_ids = request_ids // (N_NB * REQ_DEV)
    block_ids = (group_ids * (N_NB * DB_DEV) + nbr_block).astype(jnp.int32)
    nbr_rows = database.reshape(-1, BLK, E)[block_ids].reshape(SPANS, K * R, E)
    memory_spans = memory.reshape(SPANS, SPAN, 2, EH * HD)
    gain_row = enc_gain.astype(jnp.float32)

    def encode_span(operands):
        rows_in, memory_c, offset_c = operands
        wide = rows_in.astype(jnp.float32)
        normed = wide * lax.rsqrt(lax.optimization_barrier(jnp.mean(wide * wide, axis=1, keepdims=True)) + 1e-06) * gain_row
        enc_q = (jnp.dot(normed.astype(jnp.bfloat16), enc_query, preferred_element_type=jnp.float32) * score_scale).astype(jnp.bfloat16)
        enc_q = enc_q.reshape(K * R, EH, HD).astype(jnp.float32)
        key_rows = memory_c[:, 0].reshape(SPAN, EH, HD).astype(jnp.float32)
        value_rows = memory_c[:, 1].reshape(SPAN, EH, HD).astype(jnp.float32)
        scores = jnp.einsum('nhd,khd->hnk', enc_q, key_rows)
        allowed = (jnp.arange(SPAN, dtype=jnp.int32) < offset_c)[None, None, :]
        scores = jnp.where(allowed, scores, masked_score)
        row_max = lax.optimization_barrier(jnp.max(scores, axis=2, keepdims=True))
        weights = jnp.where(allowed, jnp.exp(scores - row_max), 0.0)
        totals = lax.optimization_barrier(jnp.sum(weights, axis=2))
        context = jnp.einsum('hnk,khd->nhd', weights.astype(jnp.bfloat16).astype(jnp.float32), value_rows)
        context = (context / totals.T[:, :, None]).astype(jnp.bfloat16).reshape(K * R, EH * HD)
        return (wide + jnp.dot(context, enc_out, preferred_element_type=jnp.float32)).astype(jnp.bfloat16)
    encoded = lax.map(encode_span, (nbr_rows, memory_spans, span_offset))
    weight_kv = cca_kv.reshape(E, 2 * HEADS * HD)

    def project_span(rows_in):
        return jnp.dot(rows_in, weight_kv, preferred_element_type=jnp.float32).astype(jnp.bfloat16)
    span_kv = lax.map(project_span, encoded).reshape(SPANS, K * R, 2, HEADS, HD)
    earlier_kv = jnp.concatenate([jnp.zeros_like(span_kv[:1]), span_kv[:-1]], axis=0)
    cross_queries = q_cca.reshape(SPANS, SPAN, HEADS, HD).astype(jnp.float32)

    def cross_span(operands):
        query_c, own_kv, prior_kv, offset_c = operands

        def attend_set(kv_set):
            key_rows = kv_set[:, 0].astype(jnp.float32)
            value_rows = kv_set[:, 1].astype(jnp.float32)
            scores = jnp.einsum('chd,khd->hck', query_c, key_rows) * score_scale
            row_max = lax.optimization_barrier(jnp.max(scores, axis=2, keepdims=True))
            weights = jnp.exp(scores - row_max)
            totals = lax.optimization_barrier(jnp.sum(weights, axis=2))
            summed = jnp.einsum('hck,khd->chd', weights.astype(jnp.bfloat16).astype(jnp.float32), value_rows)
            return summed / totals.T[:, :, None]
        see_own = (jnp.arange(SPAN, dtype=jnp.int32) >= offset_c)[:, None, None]
        return jnp.where(see_own, attend_set(own_kv), attend_set(prior_kv))
    cca_out = lax.map(cross_span, (cross_queries, span_kv, earlier_kv, span_offset))
    cca_out = cca_out.reshape(TOKENS, HEADS * HD)
    return (self_out + cca_out).astype(jnp.bfloat16)
```

```python
import jax
import jax.numpy as jnp
from jax import lax
from jax.experimental import pallas as pl
from jax.experimental.pallas import tpu as pltpu
from jax.sharding import Mesh, PartitionSpec as P

HD = 128
E = 2048
SPAN = 64
ROWS = 256
BLK = 16
DB_DEV = 16
LOG2E = 1.4426950408889634
SCALE = HD ** (-0.5)
MASKED = -1e30
BF = jnp.bfloat16
F32 = jnp.float32

VMEM = pl.BlockSpec(memory_space=pltpu.VMEM)
SMEM = pl.BlockSpec(memory_space=pltpu.SMEM)
ANY = pl.BlockSpec(memory_space=pl.ANY)


def dot(a, b):
    return jnp.dot(a, b, preferred_element_type=F32)


def dot_t(a, b):
    return lax.dot_general(a, b, (((1,), (1,)), ((), ())), preferred_element_type=F32)


def params(mib):
    return pltpu.CompilerParams(vmem_limit_bytes=mib << 20)


def pack_kernel(q, k, v, qo, kvo):
    for half in range(2):
        rows = slice(half * 128, half * 128 + 128)
        for j in range(4):
            cols = slice(j * 128, j * 128 + 128)
            qo[half, j] = q[rows, cols]
            kvo[half, j, 0] = k[rows, cols]
            kvo[half, j, 1] = v[rows, cols]


def pack(q, k, v):
    return pl.pallas_call(
        pack_kernel,
        out_shape=(
            jax.ShapeDtypeStruct((2, 4, 128, 128), BF),
            jax.ShapeDtypeStruct((2, 4, 2, 128, 128), BF),
        ),
        in_specs=[VMEM] * 3,
        out_specs=(VMEM, VMEM),
        name="pack",
    )(q, k, v)


def flash_step(q, keys, values, state, mask=None):
    s = dot_t(q, keys) * (SCALE * LOG2E)
    if mask is not None:
        s = jnp.where(mask, s, MASKED)
    top = jnp.max(s, axis=1, keepdims=True)
    if state is None:
        new_max = top
    else:
        old_max, old_sum, acc = state
        new_max = jnp.maximum(old_max, top)
    p = jnp.exp2(s - new_max)
    total = jnp.sum(p, axis=1, keepdims=True)
    out = dot(p.astype(BF), values)
    if state is None:
        return new_max, total, out
    shrink = jnp.exp2(old_max - new_max)
    return new_max, old_sum * shrink + total, acc * shrink + out


def near_kernel(core, q, kv, sib, acc_o, m_o, l_o):
    c = core[0]
    row = lax.broadcasted_iota(jnp.int32, (128, 256), 0)
    col = lax.broadcasted_iota(jnp.int32, (128, 256), 1)
    mask = jnp.where(col < 128, (col <= row).astype(jnp.int32), c) > 0
    for z in range(8):
        qz = q[z]
        state = flash_step(
            qz,
            jnp.concatenate([kv[z, 0], sib[z, 0]], axis=0),
            jnp.concatenate([kv[z, 1], sib[z, 1]], axis=0),
            None,
            mask,
        )
        for lo in range(0, z, 2):
            hi = min(lo + 2, z)
            keys = [r[t, 0] for t in range(lo, hi) for r in (kv, sib)]
            values = [r[t, 1] for t in range(lo, hi) for r in (kv, sib)]
            state = flash_step(
                qz, jnp.concatenate(keys, axis=0), jnp.concatenate(values, axis=0), state
            )
        m_o[z] = jnp.broadcast_to(state[0], (128, 128))
        l_o[z] = jnp.broadcast_to(state[1], (128, 128))
        acc_o[z] = state[2]


def near(core, q, kv, sib):
    f = jax.ShapeDtypeStruct((8, 128, 128), F32)
    return pl.pallas_call(
        near_kernel,
        out_shape=(f, f, f),
        in_specs=[SMEM] + [VMEM] * 3,
        out_specs=(VMEM, VMEM, VMEM),
        compiler_params=params(40),
        name="near",
    )(core, q, kv, sib)


def far_kernel(where, q, kv, sib, acc_i, m_i, l_i, out, acc_s, m_s, l_s):
    y = where[0]
    acc_s[...] = acc_i[...]
    m_s[...] = m_i[...]
    l_s[...] = l_i[...]

    def visit(block, carry):
        def rows(i, carry):
            at = pl.ds(i * 2, 2)
            qi = q[at].reshape(256, 128)
            state = (
                m_s[at].reshape(256, 128)[:, :1],
                l_s[at].reshape(256, 128)[:, :1],
                acc_s[at].reshape(256, 128),
            )
            for lo in range(0, 8, 2):
                keys = [r[block, t, 0] for t in (lo, lo + 1) for r in (kv, sib)]
                values = [r[block, t, 1] for t in (lo, lo + 1) for r in (kv, sib)]
                state = flash_step(
                    qi, jnp.concatenate(keys, axis=0), jnp.concatenate(values, axis=0), state
                )
            m_s[at] = jnp.broadcast_to(state[0], (256, 128)).reshape(2, 128, 128)
            l_s[at] = jnp.broadcast_to(state[1], (256, 128)).reshape(2, 128, 128)
            acc_s[at] = state[2].reshape(2, 128, 128)
            return carry

        return lax.fori_loop(0, 4, rows, carry)

    lax.fori_loop(0, y, visit, 0)
    out[...] = (acc_s[...] / l_s[...]).astype(BF)


def far(where, q, kv, sib, acc, m, l):
    f = pltpu.VMEM((8, 128, 128), F32)
    return pl.pallas_call(
        far_kernel,
        out_shape=jax.ShapeDtypeStruct((8, 128, 128), BF),
        in_specs=[SMEM] + [VMEM] * 6,
        out_specs=VMEM,
        scratch_shapes=[f, f, f],
        compiler_params=params(40),
        name="far",
    )(where, q, kv, sib, acc, m, l)


def encode_kernel(
    src, blk, off, own, sib, encq, gain, mem_k, mem_v, x, ctx, sems
):
    def fetch(i, carry):
        def copy(ref):
            pltpu.make_async_copy(
                ref.at[pl.ds(pl.multiple_of(blk[i] * BLK, BLK), BLK)],
                x.at[pl.ds(pl.multiple_of(i * BLK, BLK), BLK)],
                sems.at[i],
            ).start()

        @pl.when(src[i] == 0)
        def _():
            copy(own)

        @pl.when(src[i] != 0)
        def _():
            copy(sib)

        return carry

    lax.fori_loop(0, 64, fetch, 0)
    for span in range(4):
        for i in range(span * 16, span * 16 + 16):
            pltpu.make_async_copy(
                own.at[pl.ds(0, BLK)], x.at[pl.ds(i * BLK, BLK)], sems.at[i]
            ).wait()
        rows = slice(span * ROWS, span * ROWS + ROWS)
        wide = x[rows].astype(F32)
        mean = jnp.mean(wide * wide, axis=1, keepdims=True)
        h = (wide * lax.rsqrt(mean + 1e-6) * gain[...]).astype(BF)
        eq = (dot(h, encq[...]) * SCALE).astype(BF)
        tokens = slice(span * SPAN, span * SPAN + SPAN)
        s = dot_t(eq, mem_k[tokens])
        seen = lax.broadcasted_iota(jnp.int32, (ROWS, SPAN), 1) < off[span]
        s = jnp.where(seen, s, MASKED)
        top = jnp.max(s, axis=1, keepdims=True)
        p = jnp.where(seen, jnp.exp(s - top), 0.0)
        total = jnp.sum(p, axis=1, keepdims=True)
        ctx[rows] = (dot(p.astype(BF), mem_v[tokens]) / total).astype(BF)


def encode(src, blk, off, own, sib, encq, gain, mem_k, mem_v):
    return pl.pallas_call(
        encode_kernel,
        out_shape=(
            jax.ShapeDtypeStruct((1024, E), BF),
            jax.ShapeDtypeStruct((1024, 128), BF),
        ),
        in_specs=[SMEM] * 3 + [ANY] * 2 + [VMEM] * 4,
        out_specs=(VMEM, VMEM),
        scratch_shapes=[pltpu.SemaphoreType.DMA((64,))],
        compiler_params=params(48),
        name="encode",
    )(src, blk, off, own, sib, encq, gain, mem_k, mem_v)


def attend(q, keys, values):
    s = dot_t(q, keys) * (SCALE * LOG2E)
    p = jnp.exp2(s - jnp.max(s, axis=1, keepdims=True))
    return dot(p.astype(BF), values) / jnp.sum(p, axis=1, keepdims=True)


def cross_body(spans, kvx, ctx_own, ctx_sib, w2, q, qn, core, own_o, ear_o):
    c = core[0]
    for at, span in enumerate(spans):
        rows = slice(span * ROWS, span * ROWS + ROWS)
        kv = kvx[slice(at * ROWS, at * ROWS + ROWS)]
        for xx in range(4):
            for ref, cc in ((ctx_own, c), (ctx_sib, 1 - c)):
                w = w2[xx, pl.ds(pl.multiple_of(cc * 128, 128), 128)]
                kv = kv + dot(ref[xx, rows], w)
        kv = kv.astype(BF)
        mine = q[span * SPAN : span * SPAN + SPAN]
        later = qn[...] if span == 3 else q[(span + 1) * SPAN : (span + 2) * SPAN]
        both = jnp.concatenate([mine, later], axis=0)
        for j in range(4):
            cols = slice(j * 128, j * 128 + 128)
            out = attend(both[:, cols], kv[:, cols], kv[:, 512 + j * 128 : 640 + j * 128])
            own_o[at * SPAN : at * SPAN + SPAN, cols] = out[:SPAN]
            ear_o[at * SPAN : at * SPAN + SPAN, cols] = out[SPAN:]


def cross(spans, kvx, ctx_own, ctx_sib, w2, q, qn, core):
    def body(kvx, ctx_own, ctx_sib, w2, q, qn, core, own_o, ear_o):
        cross_body(spans, kvx, ctx_own, ctx_sib, w2, q, qn, core, own_o, ear_o)

    o = jax.ShapeDtypeStruct((len(spans) * SPAN, 512), F32)
    kv_block = pl.BlockSpec(
        (len(spans) * ROWS, 1024), (lambda i: (3, 0)) if spans[0] == 3 else (lambda i: (0, 0))
    )

    def whole(a):
        return pl.BlockSpec(a.shape, lambda i: (0,) * a.ndim)

    return pl.pallas_call(
        body,
        out_shape=(o, o),
        grid=(1,),
        in_specs=[kv_block] + [whole(a) for a in (ctx_own, ctx_sib, w2, q, qn)] + [SMEM],
        out_specs=(whole(o), whole(o)),
        compiler_params=params(48),
        name="cross",
    )(kvx, ctx_own, ctx_sib, w2, q, qn, core)


def final_kernel(off, attn, own_a, own_b, ear_a, recv, out):
    pos = lax.broadcasted_iota(jnp.int32, (SPAN, 512), 0)
    for span in range(4):
        own = own_b[...] if span == 3 else own_a[span * SPAN : span * SPAN + SPAN]
        ear = recv[...] if span == 0 else ear_a[(span - 1) * SPAN : span * SPAN]
        cca = jnp.where(pos >= off[span], own, ear)
        rows = slice((span % 2) * SPAN, (span % 2) * SPAN + SPAN)
        self_out = jnp.concatenate([attn[span // 2, j, rows] for j in range(4)], axis=1)
        out[span * SPAN : span * SPAN + SPAN] = (self_out.astype(F32) + cca).astype(BF)


def final(off, attn, own_a, own_b, ear_a, recv):
    return pl.pallas_call(
        final_kernel,
        out_shape=jax.ShapeDtypeStruct((256, 512), BF),
        in_specs=[SMEM] + [VMEM] * 5,
        out_specs=VMEM,
        name="final",
    )(off, attn, own_a, own_b, ear_a, recv)


def swap(a, axis):
    return lax.all_to_all(a, axis, split_axis=0, concat_axis=0, tiled=True)


def spread(a, axis):
    n = lax.axis_size(axis)
    return swap(jnp.broadcast_to(a[None], (n, *a.shape)), axis)


def sibling(a):
    return lax.ppermute(a, "c", [(0, 1), (1, 0)])


def local(
    q_self, k_self, v_self, q_cca, memory, database, nbr_block, span_offset,
    enc_query, enc_out, enc_gain, cca_kv,
):
    y, x, c = lax.axis_index("y"), lax.axis_index("x"), lax.axis_index("c")
    core = c.astype(jnp.int32).reshape(1)
    nb = 2 * x + c
    steps = lax.axis_size("y") * lax.axis_size("z")

    ids = spread(nbr_block, ("x", "c")).reshape(-1)
    db_own = spread(database, "x").reshape(-1, E)

    q_out, kv_out = pack(q_self, k_self, v_self)
    kv = swap(swap(kv_out, "c").reshape(8, 2, 128, 128), "z")
    q = swap(swap(q_out, "c").reshape(8, 128, 128), "z")

    encq = spread(lax.dynamic_slice(enc_query, (0, nb * HD), (64, HD)), ("y", "z"))
    encq = encq.reshape(E, HD)
    qn = lax.ppermute(q_cca[:SPAN], ("y", "z"), [(i, i - 1) for i in range(1, steps)])

    weight = cca_kv.reshape(E, 1024)
    w2 = dot(enc_out, weight).astype(BF)
    w2 = spread(spread(w2, "z").reshape(256, 1024), "y")

    near_out = near(core, q, kv, sibling(kv))
    kv_all = spread(kv, "y")
    attn = far(y.astype(jnp.int32).reshape(1), q, kv_all, sibling(kv_all), *near_out)

    db_sib = sibling(db_own)
    owner = ids // DB_DEV
    src = (owner % 2 != c).astype(jnp.int32)
    blk = (owner // 2) * DB_DEV + ids % DB_DEV
    mem = lax.dynamic_slice(memory, (0, 0, nb * HD), (256, 2, HD))
    rows, ctx = encode(
        src, blk, span_offset, db_own, db_sib, encq, enc_gain.reshape(1, E), mem[:, 0], mem[:, 1]
    )
    ctx_own = spread(ctx, "x")
    kvx = dot(rows, weight)
    ctx_sib = sibling(ctx_own)

    own_b, rem = cross((3,), kvx, ctx_own, ctx_sib, w2, q_cca, qn, core)
    recv = lax.ppermute(rem, ("y", "z"), [(i, i + 1) for i in range(steps - 1)])
    own_a, ear_a = cross((0, 1, 2), kvx, ctx_own, ctx_sib, w2, q_cca, qn, core)

    back = swap(swap(attn, "z").reshape(2, 4, 128, 128), "c")
    return final(span_offset, back, own_a, own_b, ear_a, recv)


def solution(mesh):
    fine = Mesh(mesh.devices.reshape(4, 8, 4, 2), ("y", "z", "x", "c"))
    s, n = ("y", "z"), ("x", "c")
    in_specs = (
        P(s, n), P(s, n), P(s, n), P(s, n),
        P(s, None, None),
        P((*s, *n), None),
        P((*s, *n)),
        P(s),
        P(s, None),
        P(s, None),
        P(),
        P(None, None, n),
    )
    return jax.shard_map(local, mesh=fine, in_specs=in_specs, out_specs=P(s, n), check_vma=False)
```

```python
import jax
import jax.numpy as jnp
from jax import lax
from jax.experimental import pallas as pl
from jax.experimental.pallas import tpu as pltpu
from jax.sharding import Mesh, PartitionSpec as P


HD = 128
E = 2048
SPAN = 64
ROWS = 256
BLK = 16
DB_DEV = 16
LOG2E = 1.4426950408889634
SCALE = HD ** (-0.5)
MASKED = -1e30
BF = jnp.bfloat16
F32 = jnp.float32

VMEM = pl.BlockSpec(memory_space=pltpu.VMEM)
SMEM = pl.BlockSpec(memory_space=pltpu.SMEM)
ANY = pl.BlockSpec(memory_space=pl.ANY)


def dot(a, b):
    return jnp.dot(a, b, preferred_element_type=F32)


def dot_t(a, b):
    return lax.dot_general(a, b, (((1,), (1,)), ((), ())), preferred_element_type=F32)


def params(mib):
    return pltpu.CompilerParams(vmem_limit_bytes=mib << 20)


def pack_kernel(where, q, k, v, keep, send):
    c = where[2]
    for out, half in ((keep, c), (send, 1 - c)):
        rows = pl.ds(pl.multiple_of(half * 128, 128), 128)
        for j in range(4):
            cols = slice(j * 128, j * 128 + 128)
            out[j, 0] = q[rows, cols]
            out[j, 1] = k[rows, cols]
            out[j, 2] = v[rows, cols].T


def pack(where, q, k, v):
    o = jax.ShapeDtypeStruct((4, 3, 128, 128), BF)
    return pl.pallas_call(
        pack_kernel,
        out_shape=(o, o),
        in_specs=[SMEM] + [VMEM] * 3,
        out_specs=(VMEM, VMEM),
        name="pack",
    )(where, q, k, v)


def flash_step(keys, values, q, state, mask=None):
    s = dot_t(keys, q)
    if mask is not None:
        s = jnp.where(mask, s, MASKED)
    top = jnp.max(s, axis=0, keepdims=True)
    if state is None:
        new_max = top
    else:
        old_max, old_sum, acc = state
        new_max = jnp.maximum(old_max, top)
    p = jnp.exp2((s - new_max) * (SCALE * LOG2E))
    total = jnp.sum(p, axis=0, keepdims=True)
    out = dot(values, p.astype(BF))
    if state is None:
        return new_max, total, out
    shrink = jnp.exp2((old_max - new_max) * (SCALE * LOG2E))
    return new_max, old_sum * shrink + total, acc * shrink + out


def tiles(refs, places):
    keys = jnp.concatenate([ref[t, 0] for t in places for ref in refs], axis=0)
    values = jnp.concatenate([ref[t, 1] for t in places for ref in refs], axis=1)
    return keys, values


def near_kernel(where, q, kv, sib, acc_o, m_o, l_o):
    c = where[2]
    row = lax.broadcasted_iota(jnp.int32, (256, 128), 0)
    col = lax.broadcasted_iota(jnp.int32, (256, 128), 1)
    mask = jnp.where(row < 128, (row <= col).astype(jnp.int32), c) > 0
    for z in range(8):
        state = flash_step(*tiles((kv, sib), (z,)), q[z], None, mask)
        for lo in range(0, z, 2):
            state = flash_step(*tiles((kv, sib), range(lo, min(lo + 2, z))), q[z], state)
        m_o[z] = jnp.broadcast_to(state[0], (8, 128))
        l_o[z] = jnp.broadcast_to(state[1], (8, 128))
        acc_o[z] = state[2]


def near(where, q, kv, sib):
    f = jax.ShapeDtypeStruct((8, 128, 128), F32)
    g = jax.ShapeDtypeStruct((8, 8, 128), F32)
    return pl.pallas_call(
        near_kernel,
        out_shape=(f, g, g),
        in_specs=[SMEM] + [VMEM] * 3,
        out_specs=(VMEM, VMEM, VMEM),
        compiler_params=params(40),
        name="near",
    )(where, q, kv, sib)


def far_kernel(where, q, kv1, sib1, kv2, sib2, kv3, sib3, acc_i, m_i, l_i, out, acc_s, m_s, l_s):
    y = where[0]
    acc_s[...] = acc_i[...]
    m_s[...] = m_i[...]
    l_s[...] = l_i[...]
    for r, refs in enumerate(((kv1, sib1), (kv2, sib2), (kv3, sib3))):

        def row(i, carry, refs=refs):
            zs = (2 * i, 2 * i + 1)
            states = [(m_s[z][:1], l_s[z][:1], acc_s[z]) for z in zs]
            for lo in (0, 4):
                keys, values = tiles(refs, range(lo, lo + 4))
                states = [flash_step(keys, values, q[z], st) for z, st in zip(zs, states)]
            for z, state in zip(zs, states):
                m_s[z] = jnp.broadcast_to(state[0], (8, 128))
                l_s[z] = jnp.broadcast_to(state[1], (8, 128))
                acc_s[z] = state[2]
            return carry

        @pl.when(y > r)
        def _(row=row):
            lax.fori_loop(0, 4, row, 0)

    for z in range(8):
        out[z] = (acc_s[z] / l_s[z][:1]).T.astype(BF)


def far(where, q, pairs, acc, m, l):
    return pl.pallas_call(
        far_kernel,
        out_shape=jax.ShapeDtypeStruct((8, 128, 128), BF),
        in_specs=[SMEM] + [VMEM] * 10,
        out_specs=VMEM,
        scratch_shapes=[
            pltpu.VMEM((8, 128, 128), F32),
            pltpu.VMEM((8, 8, 128), F32),
            pltpu.VMEM((8, 8, 128), F32),
        ],
        compiler_params=params(40),
        name="far",
    )(where, q, *pairs, acc, m, l)


def prep_kernel(enc_out, weight, encq, out):
    w2 = dot(enc_out[...], weight[...]).astype(BF)
    eq = jnp.concatenate([encq[j * 8 : j * 8 + 8] for j in range(8)], axis=1)
    for z in range(8):
        out[z, :32] = w2
        out[z, 32:] = eq


def prep(enc_out, weight, encq):
    return pl.pallas_call(
        prep_kernel,
        out_shape=jax.ShapeDtypeStruct((8, 40, 1024), BF),
        in_specs=[VMEM] * 3,
        out_specs=VMEM,
        compiler_params=params(24),
        name="prep",
    )(enc_out, weight, encq)


def gather_kernel(src, blk, *refs):
    blocks, x = refs[:8], refs[8]

    def fetch(i, carry):
        def copy(ref):
            at = pl.ds(pl.multiple_of(blk[i] * BLK, BLK), BLK)
            x[pl.ds(pl.multiple_of(i * BLK, BLK), BLK)] = ref[at]

        for side in range(2):

            @pl.when((src[i] >= 4) == (side == 1))
            def _(side=side):
                for a in range(4):

                    @pl.when(src[i] == side * 4 + a)
                    def _(a=a):
                        copy(blocks[side * 4 + a])

        return carry

    lax.fori_loop(0, 64, fetch, 0)


def gather(src, blk, blocks):
    return pl.pallas_call(
        gather_kernel,
        out_shape=jax.ShapeDtypeStruct((1024, E), BF),
        in_specs=[SMEM] * 2 + [VMEM] * 8,
        out_specs=VMEM,
        compiler_params=params(24),
        name="gather",
    )(src, blk, *blocks)


def encode_kernel(off, where, x, e0, e1, e2, e3, gain, mem_k, mem_v, ctx, encq):
    y = where[0]
    for r, ref in enumerate((e0, e1, e2, e3)):
        for z in range(8):
            for j in range(8):
                piece = ref[z, 32:, j * 128 : j * 128 + 128]
                encq[lax.rem(y + 4 - r, 4), z * 64 + j * 8 : z * 64 + j * 8 + 8] = piece

    def encode_span(span, carry):
        rows = pl.ds(pl.multiple_of(span * ROWS, ROWS), ROWS)
        wide = x[rows].astype(F32)
        mean = jnp.mean(wide * wide, axis=1, keepdims=True)
        h = (wide * lax.rsqrt(mean + 1e-6) * gain[...]).astype(BF)
        eq = (dot(h, encq[...].reshape(E, HD)) * SCALE).astype(BF)
        tokens = pl.ds(pl.multiple_of(span * SPAN, SPAN), SPAN)
        s = dot_t(eq, mem_k[tokens])
        seen = lax.broadcasted_iota(jnp.int32, (ROWS, SPAN), 1) < off[span]
        s = jnp.where(seen, s, MASKED)
        top = jnp.max(s, axis=1, keepdims=True)
        p = jnp.where(seen, jnp.exp(s - top), 0.0)
        total = jnp.sum(p, axis=1, keepdims=True)
        ctx[rows] = (dot(p.astype(BF), mem_v[tokens]) / total).astype(BF)
        return carry

    lax.fori_loop(0, 4, encode_span, 0)


def encode(off, where, x, encq, gain, mem_k, mem_v):
    return pl.pallas_call(
        encode_kernel,
        out_shape=jax.ShapeDtypeStruct((1024, 128), BF),
        in_specs=[SMEM] * 2 + [VMEM] * 8,
        out_specs=VMEM,
        scratch_shapes=[pltpu.VMEM((4, 512, 128), BF)],
        compiler_params=params(24),
        name="encode",
    )(off, where, x, *encq, gain, mem_k, mem_v)


def attend(q, keys, values):
    s = dot_t(q, keys) * (SCALE * LOG2E)
    p = jnp.exp2(s - jnp.max(s, axis=1, keepdims=True))
    return dot(p.astype(BF), values) / jnp.sum(p, axis=1, keepdims=True)


def cross_body(spans, where, kvx, ctx, w2s, q, qn, own_o, ear_o, w2):
    y, x, c = where[0], where[1], where[2]
    for turned in range(4):
        r = lax.rem(x - y + turned + 4, 4)
        for side, cc in ((0, c), (1, 1 - c)):
            for z in range(4):
                w2[side, r, z * 32 : z * 32 + 32] = w2s[turned][4 * cc + z, :32]

    def cross_span(at, carry):
        span = spans[0] + at
        rows = pl.ds(pl.multiple_of(span * ROWS, ROWS), ROWS)
        context = jnp.concatenate([ref[rows] for ref in ctx], axis=1)
        kv = kvx[pl.ds(pl.multiple_of(at * ROWS, ROWS), ROWS)]
        kv = (kv + dot(context, w2[...].reshape(1024, 1024))).astype(BF)
        mine = q[pl.ds(pl.multiple_of(span * SPAN, SPAN), SPAN)]
        if spans[0] == 3:
            later = qn[...]
        else:
            later = q[pl.ds(pl.multiple_of((span + 1) * SPAN, SPAN), SPAN)]
        both = jnp.concatenate([mine, later], axis=0)
        at_rows = pl.ds(pl.multiple_of(at * SPAN, SPAN), SPAN)
        for j in range(4):
            cols = slice(j * 128, j * 128 + 128)
            out = attend(both[:, cols], kv[:, cols], kv[:, 512 + j * 128 : 640 + j * 128])
            own_o[at_rows, cols] = out[:SPAN]
            ear_o[at_rows, cols] = out[SPAN:]
        return carry

    lax.fori_loop(0, len(spans), cross_span, 0)


def cross(spans, where, kvx, ctx, w2s, q, qn):
    def body(where, kvx, *refs):
        cross_body(spans, where, kvx, refs[:8], refs[8:12], *refs[12:])

    o = jax.ShapeDtypeStruct((len(spans) * SPAN, 512), F32)
    kv_block = pl.BlockSpec(
        (len(spans) * ROWS, 1024), (lambda i: (3, 0)) if spans[0] == 3 else (lambda i: (0, 0))
    )

    def whole(a):
        return pl.BlockSpec(a.shape, lambda i: (0,) * a.ndim)

    return pl.pallas_call(
        body,
        out_shape=(o, o),
        grid=(1,),
        in_specs=[SMEM, kv_block] + [whole(a) for a in (*ctx, *w2s, q, qn)],
        out_specs=(whole(o), whole(o)),
        scratch_shapes=[pltpu.VMEM((2, 4, 128, 1024), BF)],
        compiler_params=params(40),
        name="cross",
    )(where, kvx, *ctx, *w2s, q, qn)


def final_kernel(off, attn, own_a, own_b, ear_a, recv, out):
    pos = lax.broadcasted_iota(jnp.int32, (SPAN, 512), 0)
    for span in range(4):
        own = own_b[...] if span == 3 else own_a[span * SPAN : span * SPAN + SPAN]
        ear = recv[...] if span == 0 else ear_a[(span - 1) * SPAN : span * SPAN]
        cca = jnp.where(pos >= off[span], own, ear)
        rows = slice((span % 2) * SPAN, (span % 2) * SPAN + SPAN)
        self_out = jnp.concatenate([attn[span // 2, j, rows] for j in range(4)], axis=1)
        out[span * SPAN : span * SPAN + SPAN] = (self_out.astype(F32) + cca).astype(BF)


def final(off, attn, own_a, own_b, ear_a, recv):
    return pl.pallas_call(
        final_kernel,
        out_shape=jax.ShapeDtypeStruct((256, 512), BF),
        in_specs=[SMEM] + [VMEM] * 5,
        out_specs=VMEM,
        name="final",
    )(off, attn, own_a, own_b, ear_a, recv)


def swap(a, axis):
    return lax.all_to_all(a, axis, split_axis=0, concat_axis=0, tiled=True)


def sibling(a):
    return lax.ppermute(a, "c", [(0, 1), (1, 0)])


def turn(a, axis, distance):
    n = lax.axis_size(axis)
    return lax.ppermute(a, axis, [(i, (i + distance) % n) for i in range(n)])


def onward(a, axis, distance):
    n = lax.axis_size(axis)
    return lax.ppermute(a, axis, [(i, i + distance) for i in range(n - distance)])


def block(
    q_self, k_self, v_self, q_cca, memory, database, nbr_block, span_offset,
    enc_query, enc_out, enc_gain, cca_kv,
):
    y, x, c = lax.axis_index("y"), lax.axis_index("x"), lax.axis_index("c")
    where = jnp.stack([y, x, c]).astype(jnp.int32)
    nb = 2 * x + c
    steps = lax.axis_size("y") * lax.axis_size("z")

    pair = jnp.stack([nbr_block, sibling(nbr_block)])
    keep, send = pack(where, q_self, k_self, v_self)
    send = sibling(send)
    first, second = jnp.where(c == 0, keep, send), jnp.where(c == 0, send, keep)
    qkv = jnp.concatenate([first, second])
    pairs = jnp.stack([pair] + [turn(pair, "x", r) for r in (1, 2, 3)])
    blocks = [database] + [turn(database, "x", r) for r in (1, 2, 3)]
    blocks = blocks + [sibling(database)]
    blocks = blocks + [sibling(b) for b in blocks[1:4]]
    qn = lax.ppermute(q_cca[:SPAN], ("y", "z"), [(i, i - 1) for i in range(1, steps)])

    qkv = swap(qkv, "z")
    weight = cca_kv.reshape(E, 1024)
    encq = lax.dynamic_slice(enc_query, (0, nb * HD), (64, HD))
    bundle = prep(enc_out, weight, encq)
    qkv, bundle = lax.optimization_barrier((qkv, bundle))
    q, kv = qkv[:, 0], qkv[:, 1:]
    kvs = [kv] + [onward(kv, "y", r) for r in (1, 2, 3)]
    sibs = [sibling(kv)]
    sibs = sibs + [sibling(a) for a in kvs[1:]]

    bundle = swap(bundle, "z")
    bundles = [bundle] + [turn(bundle, "y", r) for r in (1, 2, 3)]

    near_out = near(where, q, kv, sibs[0])
    pairs, qn, _ = lax.optimization_barrier((pairs, qn, near_out[1]))
    ours = jnp.arange(4, dtype=jnp.int32)
    ids = pairs[(x - ours) % 4]
    ids = jnp.where(c == 0, ids, ids[:, ::-1]).reshape(-1)
    owner = ids // DB_DEV
    slot = ids % DB_DEV
    src = (x - owner // 2) % 4 + 4 * (owner % 2 != c)
    rows = gather(src.astype(jnp.int32), slot.astype(jnp.int32), blocks)
    kvx = dot(rows, weight)

    mem = lax.dynamic_slice(memory, (0, 0, nb * HD), (256, 2, HD))
    ctx = encode(span_offset, where, rows, bundles, enc_gain.reshape(1, E), mem[:, 0], mem[:, 1])
    ctxs = [ctx] + [turn(ctx, "x", r) for r in (1, 2, 3)]
    ctxs = ctxs + [sibling(ctx)]
    ctxs = ctxs + [sibling(a) for a in ctxs[1:4]]
    halves = [a for r in (1, 2, 3) for a in (kvs[r], sibs[r])]
    attn = far(where, q, halves, *near_out)
    back = swap(attn, "z").reshape(2, 4, 128, 128)
    own_b, rem = cross((3,), where, kvx, ctxs, bundles, q_cca, qn)
    recv = lax.ppermute(rem, ("y", "z"), [(i, i + 1) for i in range(steps - 1)])
    back = swap(back, "c")
    own_a, ear_a = cross((0, 1, 2), where, kvx, ctxs, bundles, q_cca, qn)
    return final(span_offset, back, own_a, own_b, ear_a, recv)


def solution(mesh):
    fine = Mesh(mesh.devices.reshape(4, 8, 4, 2), ("y", "z", "x", "c"))
    s, n = ("y", "z"), ("x", "c")
    in_specs = (
        P(s, n), P(s, n), P(s, n), P(s, n),
        P(s, None, None),
        P((*s, *n), None),
        P((*s, *n)),
        P(s),
        P(s, None),
        P(s, None),
        P(),
        P(None, None, n),
    )
    return jax.shard_map(block, mesh=fine, in_specs=in_specs, out_specs=P(s, n), check_vma=False)
```

```python
import jax
import jax.numpy as jnp
from jax import lax
from jax.experimental import pallas as pl
from jax.experimental.pallas import tpu as pltpu
from jax.sharding import Mesh, PartitionSpec as P


HD = 128
E = 2048
SPAN = 64
ROWS = 256
BLK = 16
DB_DEV = 16
LOG2E = 1.4426950408889634
SCALE = HD ** (-0.5)
MASKED = -1e30
BF = jnp.bfloat16
F32 = jnp.float32

VMEM = pl.BlockSpec(memory_space=pltpu.VMEM)
SMEM = pl.BlockSpec(memory_space=pltpu.SMEM)
ANY = pl.BlockSpec(memory_space=pl.ANY)


def dot(a, b):
    return jnp.dot(a, b, preferred_element_type=F32)


def dot_t(a, b):
    return lax.dot_general(a, b, (((1,), (1,)), ((), ())), preferred_element_type=F32)


def params(mib):
    return pltpu.CompilerParams(vmem_limit_bytes=mib << 20)


def pack_kernel(where, q, k, v, keep, send):
    c = where[2]
    for out, half in ((keep, c), (send, 1 - c)):
        rows = pl.ds(pl.multiple_of(half * 128, 128), 128)
        for j in range(4):
            cols = slice(j * 128, j * 128 + 128)
            out[j, 0] = q[rows, cols]
            out[j, 1] = k[rows, cols]
            out[j, 2] = v[rows, cols].T


def pack(where, q, k, v):
    o = jax.ShapeDtypeStruct((4, 3, 128, 128), BF)
    return pl.pallas_call(
        pack_kernel,
        out_shape=(o, o),
        in_specs=[SMEM] + [VMEM] * 3,
        out_specs=(VMEM, VMEM),
        name="pack",
    )(where, q, k, v)


def flash_step(keys, values, q, state, mask=None):
    s = dot_t(keys, q)
    if mask is not None:
        s = jnp.where(mask, s, MASKED)
    top = jnp.max(s, axis=0, keepdims=True)
    if state is None:
        new_max = top
    else:
        old_max, old_sum, acc = state
        new_max = jnp.maximum(old_max, top)
    p = jnp.exp2((s - new_max) * (SCALE * LOG2E))
    total = jnp.sum(p, axis=0, keepdims=True)
    out = dot(values, p.astype(BF))
    if state is None:
        return new_max, total, out
    shrink = jnp.exp2((old_max - new_max) * (SCALE * LOG2E))
    return new_max, old_sum * shrink + total, acc * shrink + out


def tiles(refs, places):
    keys = jnp.concatenate([ref[t, 0] for t in places for ref in refs], axis=0)
    values = jnp.concatenate([ref[t, 1] for t in places for ref in refs], axis=1)
    return keys, values


def near_kernel(where, q, kv, sib, state_o):
    c = where[2]
    row = lax.broadcasted_iota(jnp.int32, (256, 128), 0)
    col = lax.broadcasted_iota(jnp.int32, (256, 128), 1)
    mask = jnp.where(row < 128, (row <= col).astype(jnp.int32), c) > 0
    for z in range(8):
        state = flash_step(*tiles((kv, sib), (z,)), q[z], None, mask)
        for lo in range(0, z, 2):
            state = flash_step(*tiles((kv, sib), range(lo, min(lo + 2, z))), q[z], state)
        state_o[z, :128] = state[2]
        state_o[z, 128:136] = jnp.broadcast_to(state[0], (8, 128))
        state_o[z, 136:] = jnp.broadcast_to(state[1], (8, 128))


def near(where, q, kv, sib):
    return pl.pallas_call(
        near_kernel,
        out_shape=jax.ShapeDtypeStruct((8, 144, 128), F32),
        in_specs=[SMEM] + [VMEM] * 3,
        out_specs=VMEM,
        compiler_params=params(40),
        name="near",
    )(where, q, kv, sib)


def far_kernel(where, src, blk, q, *refs):
    kvs, state_i, blocks = refs[:6], refs[6], refs[7:15]
    out, x, state_s, kv_s, sib_s, sems = refs[15:]

    def fetch(i, carry):
        place, at = src[i], pl.multiple_of(blk[i] * BLK, BLK)

        def pick(lo, hi):
            if hi - lo == 1:
                pltpu.make_async_copy(
                    blocks[lo].at[pl.ds(at, BLK)],
                    x.at[pl.ds(pl.multiple_of(i * BLK, BLK), BLK)],
                    sems.at[i],
                ).start()
                return 0
            mid = (lo + hi) // 2
            return lax.cond(place < mid, lambda: pick(lo, mid), lambda: pick(mid, hi))

        return carry + pick(0, 8)

    lax.fori_loop(0, 64, fetch, 0)
    state_s[...] = state_i[...]

    def visit(r, carry):
        for i in range(3):
            kv, sib = kvs[2 * i : 2 * i + 2]

            @pl.when(r == i)
            def _(kv=kv, sib=sib):
                kv_s[...] = kv[...]
                sib_s[...] = sib[...]

        states = [
            (state_s[z, 128:129], state_s[z, 136:137], state_s[z, :128]) for z in range(8)
        ]
        for lo in (0, 4):
            keys, values = tiles((kv_s, sib_s), range(lo, lo + 4))
            states = [flash_step(keys, values, q[z], states[z]) for z in range(8)]
        for z in range(8):
            state_s[z, :128] = states[z][2]
            state_s[z, 128:136] = jnp.broadcast_to(states[z][0], (8, 128))
            state_s[z, 136:] = jnp.broadcast_to(states[z][1], (8, 128))
        return carry

    lax.fori_loop(0, where[0], visit, 0)
    for z in range(8):
        out[z] = (state_s[z, :128] / state_s[z, 136:137]).T.astype(BF)
    for i in range(64):
        rows = pl.ds(i * BLK, BLK)
        pltpu.make_async_copy(blocks[0].at[pl.ds(0, BLK)], x.at[rows], sems.at[i]).wait()


def far(where, src, blk, q, pairs, state, blocks):
    return pl.pallas_call(
        far_kernel,
        out_shape=(
            jax.ShapeDtypeStruct((8, 128, 128), BF),
            jax.ShapeDtypeStruct((1024, E), BF),
        ),
        in_specs=[SMEM] * 3 + [VMEM] * 8 + [pl.BlockSpec(memory_space=pltpu.HBM)] * 8,
        out_specs=(VMEM, pl.BlockSpec(memory_space=pltpu.HBM)),
        scratch_shapes=[
            pltpu.VMEM((8, 144, 128), F32),
            pltpu.VMEM((8, 2, 128, 128), BF),
            pltpu.VMEM((8, 2, 128, 128), BF),
            pltpu.SemaphoreType.DMA((64,)),
        ],
        compiler_params=params(20),
        name="far",
    )(where, src, blk, q, *pairs, state, *blocks)


def prep_kernel(enc_out, weight, encq, out):
    w2 = dot(enc_out[...], weight[...]).astype(BF)
    eq = jnp.concatenate([encq[j * 8 : j * 8 + 8] for j in range(8)], axis=1)
    for z in range(8):
        out[z, :32] = w2
        out[z, 32:] = eq


def prep(enc_out, weight, encq):
    return pl.pallas_call(
        prep_kernel,
        out_shape=jax.ShapeDtypeStruct((8, 40, 1024), BF),
        in_specs=[VMEM] * 3,
        out_specs=VMEM,
        compiler_params=params(24),
        name="prep",
    )(enc_out, weight, encq)


def encode_kernel(off, where, x_hbm, e0, e1, e2, e3, gain, mem_k, mem_v, ctx, encq, x, sems):
    def piece_of(span):
        rows = pl.ds(pl.multiple_of(span * ROWS, ROWS), ROWS)
        return pltpu.make_async_copy(x_hbm.at[rows], x.at[rows], sems.at[span])

    for span in range(4):
        piece_of(span).start()
    y = where[0]
    for r, ref in enumerate((e0, e1, e2, e3)):
        for z in range(8):
            for j in range(8):
                piece = ref[z, :, j * 128 : j * 128 + 128]
                encq[lax.rem(y + 4 - r, 4), z * 64 + j * 8 : z * 64 + j * 8 + 8] = piece

    def encode_span(span, carry):
        piece_of(span).wait()
        rows = pl.ds(pl.multiple_of(span * ROWS, ROWS), ROWS)
        wide = x[rows].astype(F32)
        mean = jnp.mean(wide * wide, axis=1, keepdims=True)
        h = (wide * lax.rsqrt(mean + 1e-6) * gain[...]).astype(BF)
        eq = (dot(h, encq[...].reshape(E, HD)) * SCALE).astype(BF)
        tokens = pl.ds(pl.multiple_of(span * SPAN, SPAN), SPAN)
        s = dot_t(eq, mem_k[tokens])
        seen = lax.broadcasted_iota(jnp.int32, (ROWS, SPAN), 1) < off[span]
        s = jnp.where(seen, s, MASKED)
        top = jnp.max(s, axis=1, keepdims=True)
        p = jnp.where(seen, jnp.exp(s - top), 0.0)
        total = jnp.sum(p, axis=1, keepdims=True)
        ctx[rows] = (dot(p.astype(BF), mem_v[tokens]) / total).astype(BF)
        return carry

    lax.fori_loop(0, 4, encode_span, 0)


def encode(off, where, x, encqs, gain, mem_k, mem_v):
    return pl.pallas_call(
        encode_kernel,
        out_shape=jax.ShapeDtypeStruct((1024, 128), BF),
        in_specs=[SMEM] * 2 + [pl.BlockSpec(memory_space=pltpu.HBM)] + [VMEM] * 7,
        out_specs=VMEM,
        scratch_shapes=[
            pltpu.VMEM((4, 512, 128), BF),
            pltpu.VMEM((1024, E), BF),
            pltpu.SemaphoreType.DMA((4,)),
        ],
        compiler_params=params(20),
        name="encode",
    )(off, where, x, *encqs, gain, mem_k, mem_v)


def attend(q, keys, values):
    s = dot_t(q, keys) * (SCALE * LOG2E)
    p = jnp.exp2(s - jnp.max(s, axis=1, keepdims=True))
    return dot(p.astype(BF), values) / jnp.sum(p, axis=1, keepdims=True)


def cross_kernel(off, where, kvx, *refs):
    ctx, w2s, (q, qn, cca_o, rem_o, w2, ear) = refs[:8], refs[8:12], refs[12:]
    y, x, c = where[0], where[1], where[2]
    for turned in range(4):
        r = lax.rem(x - y + turned + 4, 4)
        for side, cc in ((0, c), (1, 1 - c)):
            for z in range(4):
                w2[side, r, z * 32 : z * 32 + 32] = w2s[turned][4 * cc + z]
    pos = lax.broadcasted_iota(jnp.int32, (SPAN, HD), 0)

    def cross_span(span, carry):
        rows = pl.ds(pl.multiple_of(span * ROWS, ROWS), ROWS)
        context = jnp.concatenate([ref[rows] for ref in ctx], axis=1)
        kv = (kvx[rows] + dot(context, w2[...].reshape(1024, 1024))).astype(BF)
        at = pl.ds(pl.multiple_of(span * SPAN, SPAN), SPAN)
        after_at = pl.ds(pl.multiple_of(jnp.minimum(span + 1, 3) * SPAN, SPAN), SPAN)
        later = jnp.where(span == 3, qn[...], q[after_at])
        both = jnp.concatenate([q[at], later], axis=0)
        own_seen = (pos >= off[span]) | (span == 0)
        for j in range(4):
            cols = slice(j * 128, j * 128 + 128)
            out = attend(both[:, cols], kv[:, cols], kv[:, 512 + j * 128 : 640 + j * 128])
            cca_o[at, cols] = jnp.where(own_seen, out[:SPAN], ear[:, cols])
            ear[:, cols] = out[SPAN:]
        return carry

    ear[...] = jnp.zeros((SPAN, 512), F32)
    lax.fori_loop(0, 4, cross_span, 0)
    rem_o[...] = ear[...]


def cross(off, where, kvx, ctx, w2s, q, qn):
    return pl.pallas_call(
        cross_kernel,
        out_shape=(
            jax.ShapeDtypeStruct((256, 512), F32),
            jax.ShapeDtypeStruct((SPAN, 512), F32),
        ),
        in_specs=[SMEM] * 2 + [VMEM] * 15,
        out_specs=(VMEM, VMEM),
        scratch_shapes=[pltpu.VMEM((2, 4, 128, 1024), BF), pltpu.VMEM((SPAN, 512), F32)],
        compiler_params=params(20),
        name="cross",
    )(off, where, kvx, *ctx, *w2s, q, qn)


def final_kernel(off, attn, cca, recv, out):
    pos = lax.broadcasted_iota(jnp.int32, (SPAN, 512), 0)
    for span in range(4):
        at = slice(span * SPAN, span * SPAN + SPAN)
        add = cca[at]
        if span == 0:
            add = jnp.where(pos >= off[0], add, recv[...])
        rows = slice((span % 2) * SPAN, (span % 2) * SPAN + SPAN)
        self_out = jnp.concatenate([attn[span // 2, j, rows] for j in range(4)], axis=1)
        out[at] = (self_out.astype(F32) + add).astype(BF)


def final(off, attn, cca, recv):
    return pl.pallas_call(
        final_kernel,
        out_shape=jax.ShapeDtypeStruct((256, 512), BF),
        in_specs=[SMEM] + [VMEM] * 3,
        out_specs=VMEM,
        name="final",
    )(off, attn, cca, recv)


def swap(a, axis):
    return lax.all_to_all(a, axis, split_axis=0, concat_axis=0, tiled=True)


def sibling(a):
    return lax.ppermute(a, "c", [(0, 1), (1, 0)])


def turn(a, axis, distance):
    n = lax.axis_size(axis)
    return lax.ppermute(a, axis, [(i, (i + distance) % n) for i in range(n)])


def onward(a, axis, distance):
    n = lax.axis_size(axis)
    return lax.ppermute(a, axis, [(i, i + distance) for i in range(n - distance)])


def block(
    q_self, k_self, v_self, q_cca, memory, database, nbr_block, span_offset,
    enc_query, enc_out, enc_gain, cca_kv,
):
    y, x, c = lax.axis_index("y"), lax.axis_index("x"), lax.axis_index("c")
    where = jnp.stack([y, x, c]).astype(jnp.int32)
    nb = 2 * x + c
    steps = lax.axis_size("y") * lax.axis_size("z")

    pair = jnp.stack([nbr_block, sibling(nbr_block)])
    keep, send = pack(where, q_self, k_self, v_self)
    send = sibling(send)
    first, second = jnp.where(c == 0, keep, send), jnp.where(c == 0, send, keep)
    qkv = jnp.concatenate([first, second])
    pairs = jnp.stack([pair] + [turn(pair, "x", r) for r in (1, 2, 3)])
    cca_kv, pairs = lax.optimization_barrier((cca_kv, pairs))
    blocks = [database] + [turn(database, "x", r) for r in (1, 2, 3)]
    blocks = blocks + [sibling(database)]
    blocks = blocks + [sibling(b) for b in blocks[1:4]]
    qn = lax.ppermute(q_cca[:SPAN], ("y", "z"), [(i, i - 1) for i in range(1, steps)])

    qkv = swap(qkv, "z")
    weight = cca_kv.reshape(E, 1024)
    encq = lax.dynamic_slice(enc_query, (0, nb * HD), (64, HD))
    bundle = prep(enc_out, weight, encq)
    qkv, bundle = lax.optimization_barrier((qkv, bundle))
    q, kv = qkv[:, 0], qkv[:, 1:]
    kvs = [kv] + [onward(kv, "y", r) for r in (1, 2, 3)]
    sibs = [sibling(kv)]
    sibs = sibs + [sibling(a) for a in kvs[1:]]

    bundle = swap(bundle, "z")
    near_out = near(where, q, kv, sibs[0])
    pairs, _ = lax.optimization_barrier((pairs, near_out))
    ours = jnp.arange(4, dtype=jnp.int32)
    ids = pairs[(x - ours) % 4]
    ids = jnp.where(c == 0, ids, ids[:, ::-1]).reshape(-1)
    owner = ids // DB_DEV
    slot = (ids % DB_DEV).astype(jnp.int32)
    src = ((x - owner // 2) % 4 + 4 * (owner % 2 != c)).astype(jnp.int32)
    mem = lax.dynamic_slice(memory, (0, 0, nb * HD), (256, 2, HD))
    mem_k, mem_v = mem[:, 0], mem[:, 1]
    bundle, src, slot, mem_k, mem_v = lax.optimization_barrier((bundle, src, slot, mem_k, mem_v))
    encq, w2 = bundle[:, 32:], bundle[:, :32]
    encqs = [encq] + [turn(encq, "y", r) for r in (1, 2, 3)]
    w2s = [w2] + [turn(w2, "y", r) for r in (1, 2, 3)]

    halves = [a for r in (1, 2, 3) for a in (kvs[r], sibs[r])]
    attn, rows = far(where, src, slot, q, halves, near_out, blocks)
    ctx = encode(
        span_offset, where, rows, encqs, enc_gain.reshape(1, E), mem_k, mem_v
    )
    qn, ctx = lax.optimization_barrier((qn, ctx))
    kvx = dot(rows, weight)
    ctxs = [ctx] + [turn(ctx, "x", r) for r in (1, 2, 3)]
    ctxs = ctxs + [sibling(ctx)]
    ctxs = ctxs + [sibling(a) for a in ctxs[1:4]]
    back = swap(attn, "z").reshape(2, 4, 128, 128)
    cca, rem = cross(span_offset, where, kvx, ctxs, w2s, q_cca, qn)
    recv = lax.ppermute(rem, ("y", "z"), [(i, i + 1) for i in range(steps - 1)])
    back = swap(back, "c")
    return final(span_offset, back, cca, recv)


def solution(mesh):
    fine = Mesh(mesh.devices.reshape(4, 8, 4, 2), ("y", "z", "x", "c"))
    s, n = ("y", "z"), ("x", "c")
    in_specs = (
        P(s, n), P(s, n), P(s, n), P(s, n),
        P(s, None, None),
        P((*s, *n), None),
        P((*s, *n)),
        P(s),
        P(s, None),
        P(s, None),
        P(),
        P(None, None, n),
    )
    return jax.shard_map(block, mesh=fine, in_specs=in_specs, out_specs=P(s, n), check_vma=False)
```
